512 devices in a mesh: tm: 16 (over y, core), row: 8 (over z), col: 4 (over x).
Axes of the slice: x: 4, y: 8, z: 8, core: 2. Of those that a mesh axis runs over, the one named last changes fastest.
Arguments:
- frames: bfloat16 [256, 2, 128, 512], P('tm', None, 'row', 'col'), may hold values from -6 to 6
- phase: int32 [256], P('tm'), may hold values from 0 to 15
- shift: int32 [2, 8, 32], P(None, 'row', 'col'), may hold values from -6 to 6
- interp_rows: bfloat16 [32, 36], replicated, may hold values from -0.75 to 1.75, as said below
- interp_cols: bfloat16 [32, 36], replicated, may hold values from -0.75 to 1.75, as said below
Outputs:
- ensemble: float32 [16, 8, 32, 1024], P('tm', 'row', 'col')
The draws below stay inside these ranges and needn't reach their ends.
Inputs may be any that keep to these rules, and one draw needn't show every extreme that they name: `interp_rows`: row i is zero outside columns i to i + 4. `interp_cols`: row i is zero outside columns i to i + 4.
All inputs are finite; a program needn't handle non-finite values.
Results may differ from the reference program's by a relative error of at most 0.0077.
Values may be sent and summed in bfloat16 or wider, within the bound.
No kernel may reach another device: no remote copies, remote signals or barrier semaphores. Data moves between devices by JAX's collectives and lax.ppermute only.
A program may use at most 64 MiB of HBM per device.

```python
import math
from functools import partial
import jax
import jax.numpy as jnp
import numpy as np
from jax import lax

WIN = 32
STEP = 16
BAND = 2
DMAX = 6
HALO = 16
BINS = 16
PAIRS = 256
NR = 128
NC = 512
NWR = 8
NWC = 32


def banded_matrix(key):
    span_cols = WIN + 2 * BAND
    row_ids = jnp.arange(WIN, dtype=jnp.int32)[:, None]
    col_ids = jnp.arange(span_cols, dtype=jnp.int32)[None, :]
    offsets = col_ids - row_ids
    inside = (offsets >= 0) & (offsets <= 2 * BAND)
    values = 0.3 * jnp.clip(jax.random.normal(key, (WIN, span_cols), jnp.float32), -2.5, 2.5)
    values = values + jnp.where(offsets == BAND, 1.0, 0.0)
    return jnp.where(inside, values, 0.0).astype(jnp.float32).astype(jnp.bfloat16)


def draw_interp_rows(key, part):
    return banded_matrix(jax.random.fold_in(key, 11))


def draw_interp_cols(key, part):
    return banded_matrix(jax.random.fold_in(key, 23))


def with_ends(entries, key, low, high):
    longest = entries.shape.index(max(entries.shape))
    spots = []
    for shift in (0, 1):
        where = [jax.random.randint(jax.random.fold_in(key, axis), (), 0, length) for axis, length in enumerate(entries.shape)]
        where[longest] = (where[longest] + shift) % entries.shape[longest]
        spots.append(tuple(where))
    return entries.at[spots[0]].set(low).at[spots[1]].set(high)


def block_scale(stream_key, shape, shards, smallest, largest):
    def one(axis_at, parts):
        heights = jax.random.uniform(jax.random.fold_in(jax.random.fold_in(stream_key, 6), axis_at), (parts,), jnp.float32, smallest / len(shards), largest / len(shards))
        return jnp.repeat(jnp.exp(heights), shape[axis_at] // parts).reshape((-1,) + (1,) * (len(shape) - axis_at - 1))

    loudness = one(*shards[0])
    for cut in shards[1:]:
        loudness = loudness * one(*cut)
    return loudness


def cumulative_ranks(count, slope):
    weights = [(1 << 20) // math.isqrt(standing ** slope) + 1 for standing in range(1, count + 1)]
    deviation = 1 + sum(weights) // (1 << 30)
    return np.cumsum(np.array([max(1, weight // deviation) for weight in weights]))


def ranked_ids(rng, shape, amount, skew):
    listing = cumulative_ranks(amount, skew)
    pick = jax.random.randint(jax.random.fold_in(rng, 1), shape, 0, int(listing[amount - 1]))
    grade = jnp.searchsorted(jnp.asarray(listing, jnp.int32), pick, side="right")
    return jax.random.permutation(jax.random.fold_in(rng, 2), amount)[grade].astype(jnp.int32)


def noise(key, shape, scale, bound, cuts=(), kind=jnp.bfloat16):
    result = jax.random.normal(key, shape, jnp.float32) * scale
    if len(cuts) > 0:
        result = block_scale(key, shape, cuts, -0.22, 0.18) * result
    return jnp.clip(result, min=-bound, max=bound).astype(kind)


def setup_inputs(seed: int = 0) -> dict:
    arg_keys = jax.random.split(jax.random.key(seed), 6)
    frames = noise(arg_keys[0], (PAIRS, 2, NR, NC), 1.0, 6.0, ((0, 16), (2, 8), (3, 4)))
    phase = with_ends(ranked_ids(arg_keys[1], (PAIRS,), BINS, 2), jax.random.fold_in(arg_keys[1], 3), 0, BINS - 1).astype(jnp.int32)
    shift = with_ends(jax.random.randint(arg_keys[2], (2, NWR, NWC), -DMAX, DMAX + 1), jax.random.fold_in(arg_keys[2], 1), -DMAX, DMAX).astype(jnp.int32)
    interp_rows = draw_interp_rows(jax.random.fold_in(arg_keys[5], 71), 0)
    interp_cols = draw_interp_cols(jax.random.fold_in(arg_keys[5], 71), 0)
    return {"frames": frames, "phase": phase, "shift": shift, "interp_rows": interp_rows, "interp_cols": interp_cols}


HIGHEST_PRECISION = lax.Precision.HIGHEST


def window_cut(picture, row_start, col_start, extent):
    return lax.dynamic_slice(picture, (row_start, col_start), (extent, extent))


def cut_windows(picture, row_starts, col_starts, extent):
    return jax.vmap(partial(window_cut, extent=extent), in_axes=(None, 0, 0))(picture, row_starts, col_starts)


def angle_tables():
    indices = jnp.arange(WIN, dtype=jnp.int32)
    product = (indices[:, None] * indices[None, :]) % WIN
    angles = product.astype(jnp.float32) * (2.0 * math.pi / WIN)
    return jnp.cos(angles), jnp.sin(angles)


def forward(centred, cosine_half, sine_half):
    right_table = jnp.concatenate([cosine_half, -sine_half], axis=1)
    halved = jnp.einsum("abn,bk->akn", centred.astype(jnp.float32), right_table.astype(jnp.float32)).astype(jnp.bfloat16)
    left_table = jnp.concatenate([cosine_half, sine_half], axis=0)
    stacked = jnp.einsum("ja,akn->jkn", left_table.astype(jnp.float32), halved.astype(jnp.float32))
    real_part = stacked[:WIN, :WIN] + stacked[WIN:, WIN:]
    imag_part = stacked[:WIN, WIN:] - stacked[WIN:, :WIN]
    return real_part, imag_part


def inverse(real_part, imag_part, cosine_full, sine_full):
    section_real = jnp.einsum("jkn,kv->jvn", real_part, cosine_full, precision=HIGHEST_PRECISION) - jnp.einsum("jkn,kv->jvn", imag_part, sine_full, precision=HIGHEST_PRECISION)
    section_imag = jnp.einsum("jkn,kv->jvn", real_part, sine_full, precision=HIGHEST_PRECISION) + jnp.einsum("jkn,kv->jvn", imag_part, cosine_full, precision=HIGHEST_PRECISION)
    planes = jnp.einsum("uj,jvn->uvn", cosine_full, section_real, precision=HIGHEST_PRECISION) - jnp.einsum("uj,jvn->uvn", sine_full, section_imag, precision=HIGHEST_PRECISION)
    return planes * (1.0 / WIN ** 3)


def centre_window(values):
    return (values - jnp.mean(values, axis=(0, 1), keepdims=True)).astype(jnp.bfloat16)


def reference(frames, phase, shift, interp_rows, interp_cols):
    image_rows = frames.shape[2]
    image_cols = frames.shape[3]
    win_rows = image_rows // STEP
    win_cols = image_cols // STEP
    win_count = win_rows * win_cols
    indices = jnp.arange(win_count, dtype=jnp.int32)
    base_start = HALO - (WIN - STEP) // 2
    start_rows = (base_start + STEP * (indices // win_cols)).astype(jnp.int32)
    start_cols = (base_start + STEP * (indices % win_cols)).astype(jnp.int32)
    patch_rows = (start_rows + shift[0].reshape(-1) - BAND).astype(jnp.int32)
    patch_cols = (start_cols + shift[1].reshape(-1) - BAND).astype(jnp.int32)
    cosine_full, sine_full = angle_tables()
    cosine_half = cosine_full.astype(jnp.bfloat16)
    sine_half = sine_full.astype(jnp.bfloat16)
    rows_weight = interp_rows.astype(jnp.float32)
    cols_weight = interp_cols.astype(jnp.float32)

    def one_pair(running, inputs):
        frame_pair, bin_index = inputs
        padded = jnp.pad(frame_pair, ((0, 0), (HALO, HALO), (HALO, HALO)))
        wins_a = cut_windows(padded[0], start_rows, start_cols, WIN)
        patches = cut_windows(padded[1], patch_rows, patch_cols, WIN + 2 * BAND)
        lifted = jnp.einsum("ia,wab->wib", rows_weight, patches.astype(jnp.float32)).astype(jnp.bfloat16)
        deformed = jnp.einsum("wib,jb->ijw", lifted.astype(jnp.float32), cols_weight)
        centred_a = centre_window(jnp.transpose(wins_a, (1, 2, 0)).astype(jnp.float32))
        centred_b = centre_window(deformed)
        a_real, a_imag = forward(centred_a, cosine_half, sine_half)
        b_real, b_imag = forward(centred_b, cosine_half, sine_half)
        cross_real = a_real * b_real + a_imag * b_imag
        cross_imag = a_real * b_imag - a_imag * b_real
        real_sum, imag_sum = running
        return (real_sum.at[bin_index].add(cross_real), imag_sum.at[bin_index].add(cross_imag)), None

    zeros = jnp.zeros((BINS, WIN, WIN, win_count), jnp.float32)
    sums, _ = lax.scan(one_pair, (zeros, zeros), (frames, phase))
    real_all = jnp.transpose(sums[0], (1, 2, 0, 3)).reshape(WIN, WIN, BINS * win_count)
    imag_all = jnp.transpose(sums[1], (1, 2, 0, 3)).reshape(WIN, WIN, BINS * win_count)
    planes = inverse(real_all, imag_all, cosine_full, sine_full)
    planes = planes.reshape(WIN, WIN, BINS, win_rows, win_cols)
    return jnp.transpose(planes, (2, 3, 4, 0, 1)).reshape(BINS, win_rows, win_cols, WIN * WIN)
```

```python
import math
from functools import partial

import jax
import jax.numpy as jnp
import numpy as np
from jax import lax
from jax.experimental import pallas as pl
from jax.experimental.pallas import tpu as pltpu
from jax.sharding import PartitionSpec as P

WIN = 32
STEP = 16
BAND = 2
HALO = 16
SLOTS = WIN // 2
PATCH = WIN + 2 * BAND
SPAN = 48
GROUP = 4

F32 = jnp.float32
BF16 = jnp.bfloat16
HIGHEST = lax.Precision.HIGHEST


def dot(a, b, dims=((1,), (0,)), precision=None):
    return lax.dot_general(a, b, (dims, ((), ())), precision=precision, preferred_element_type=F32)


def tables():
    index = np.arange(WIN)
    angles = (index[:, None] * index[None, :] % WIN).astype(np.float32) * np.float32(2.0 * math.pi / WIN)
    return np.cos(angles).astype(np.float32), np.sin(angles).astype(np.float32)


def as_bf16(values):
    return np.asarray(values, np.float32).astype(jnp.bfloat16)


def constants(windows):
    cosine, sine = tables()
    cos_half = as_bf16(cosine).astype(np.float32)
    sin_half = as_bf16(sine).astype(np.float32)
    real = cos_half[:, :SLOTS]
    imag = -sin_half[:, :SLOTS]
    imag[:, 0] = cos_half[:, SLOTS]
    packed = np.concatenate([np.tile(real, (1, windows)), np.tile(imag, (1, windows))], axis=1)
    lanes = windows * SLOTS
    first = np.zeros((2 * HALO + windows * STEP, 2 * lanes), np.float32)
    for w in range(windows):
        top = HALO - (WIN - STEP) // 2 + STEP * w
        first[top : top + WIN, w * SLOTS : (w + 1) * SLOTS] = real
        first[top : top + WIN, lanes + w * SLOTS : lanes + (w + 1) * SLOTS] = imag
    rows = np.concatenate([np.tile(cos_half, (GROUP, 1)), np.tile(sin_half, (GROUP, 1))], axis=0)
    block = np.tile(np.repeat(np.arange(GROUP), WIN), 2)
    left_a = np.where(block[:, None] == np.repeat(np.arange(GROUP), WIN)[None, :], np.tile(rows, (1, GROUP)), 0.0)
    spread = np.zeros((PATCH, GROUP * SPAN), np.float32)
    for g in range(GROUP):
        spread[np.arange(PATCH), g * SPAN + np.arange(PATCH)] = 1.0
    lag = np.arange(WIN)
    back_real = 2.0 * cosine[:SLOTS]
    back_imag = -2.0 * sine[:SLOTS]
    back_real[0] = 1.0
    back_imag[0] = np.where(lag % 2 == 0, 1.0, -1.0)
    folded = np.concatenate([np.tile(back_real, (windows, 1)), np.tile(back_imag, (windows, 1))], axis=0) / WIN**3
    places = np.zeros((4, 2 * lanes, 4 * WIN), np.float32)
    for r in range(4):
        places[r, :, r * WIN : (r + 1) * WIN] = folded
    inverse_rows = np.concatenate([cosine, sine], axis=0)
    return dict(
        packed=as_bf16(packed),
        first=as_bf16(first),
        rows=as_bf16(rows),
        left_a=as_bf16(left_a),
        spread=as_bf16(spread),
        places=places,
        inverse_rows=inverse_rows,
    )


def whole(space=pltpu.VMEM):
    return pl.BlockSpec(memory_space=space)


def strips_kernel(x_ref, right_ref, left_ref):
    pairs, _, tile_rows, tile_cols = x_ref.shape
    row = lax.broadcasted_iota(jnp.int32, (2 * HALO, tile_cols), 0)
    col = lax.broadcasted_iota(jnp.int32, (2 * HALO, tile_cols), 1)
    wanted = jnp.where(row < HALO, row + (tile_cols - HALO), row - HALO)
    pick = (col == wanted).astype(F32).astype(BF16)
    span = pairs * tile_rows
    for image in range(2):
        pixels = x_ref[:, image].reshape(span, tile_cols)
        taken = dot(pick, pixels, ((1,), (1,))).astype(BF16)
        right_ref[:, image * span : (image + 1) * span] = taken[:HALO]
        left_ref[:, image * span : (image + 1) * span] = taken[HALO:]


def weights_kernel(
    shift_ref, rows_ref, cols_ref, packed_ref, table_ref, spread_ref, high_ref, low_ref, rhigh_ref, rlow_ref, wide_ref
):
    windows = shift_ref.shape[2]
    lanes = wide_ref.shape[2]
    column = dot(cols_ref[...], packed_ref[...], ((0,), (0,)))
    column = jnp.concatenate([column, jnp.zeros((40 - PATCH, 2 * lanes), F32)], axis=0)
    wide_ref[...] = jnp.zeros_like(wide_ref)
    owner = lax.broadcasted_iota(jnp.int32, (40, lanes), 1) // SLOTS
    for w in range(windows):
        start = STEP * w + HALO - (WIN - STEP) // 2 - BAND + shift_ref[1, 0, w]
        rows = pl.ds(start, 40)
        for t in range(2):
            wide_ref[t, rows, :] = jnp.where(
                owner == w, column[:, t * lanes : (t + 1) * lanes], wide_ref[t, rows, :]
            )
    total = high_ref.shape[0]
    values = jnp.concatenate([wide_ref[0, :total, :], wide_ref[1, :total, :]], axis=1)
    high = values.astype(BF16)
    high_ref[...] = high
    low_ref[...] = (values - high.astype(F32)).astype(BF16)
    spread = dot(rows_ref[...], spread_ref[...]).astype(BF16)
    left = dot(table_ref[...], spread)
    mine = (lax.broadcasted_iota(jnp.int32, left.shape, 0) // WIN) % GROUP
    theirs = lax.broadcasted_iota(jnp.int32, left.shape, 1) // SPAN
    left = jnp.where(mine == theirs, left, 0.0)
    high = left.astype(BF16)
    rhigh_ref[...] = high
    rlow_ref[...] = (left - high.astype(F32)).astype(BF16)


def spectra_kernel(
    phase_ref,
    shift_ref,
    own_ref,
    up_ref,
    down_ref,
    own_side_ref,
    up_side_ref,
    down_side_ref,
    first_ref,
    high_ref,
    low_ref,
    left_ref,
    rhigh_ref,
    rlow_ref,
    out_ref,
    half_a,
    half_b,
    sums,
):
    pairs, _, tile_rows, tile_cols = own_ref.shape
    windows = shift_ref.shape[2]
    lanes = windows * SLOTS
    span = pairs * tile_rows
    right = HALO + tile_cols

    def sides(ref, image):
        return jnp.transpose(ref[:, image * span : (image + 1) * span].astype(F32)).astype(BF16)

    def along_columns(pixels, strip, weights):
        edge = jnp.concatenate([weights[:HALO], weights[right:]], axis=0)
        return dot(pixels, weights[HALO:right]) + dot(strip, edge)

    for at, (ref, side_ref) in enumerate(
        ((up_ref, up_side_ref), (own_ref, own_side_ref), (down_ref, down_side_ref))
    ):
        place = slice(at * tile_rows, (at + 1) * tile_rows)
        pixels, strip = ref[:, 0].reshape(span, tile_cols), sides(side_ref, 0)
        half = along_columns(pixels, strip, first_ref[...])
        half_a[:, place, :] = half.reshape(pairs, tile_rows, 2 * lanes)
        pixels, strip = ref[:, 1].reshape(span, tile_cols), sides(side_ref, 1)
        half = along_columns(pixels, strip, high_ref[...]) + along_columns(pixels, strip, low_ref[...])
        for t in range(2):
            half_b[t, :, place, :] = half[:, t * lanes : (t + 1) * lanes].reshape(pairs, tile_rows, lanes)
    half_b[:, :, 3 * tile_rows :, :] = jnp.zeros((2, pairs, half_b.shape[2] - 3 * tile_rows, lanes), F32)
    sums[...] = jnp.zeros_like(sums)

    head = tile_rows - (WIN - STEP) // 2
    zero_slot = lax.broadcasted_iota(jnp.int32, (1, lanes), 1) % SLOTS == 0
    owner = lax.broadcasted_iota(jnp.int32, (1, lanes), 1) // SLOTS
    first_row = lax.broadcasted_iota(jnp.int32, (GROUP * WIN, 1), 0) % WIN == 0
    offsets = [HALO - (WIN - STEP) // 2 - BAND + shift_ref[0, 0, w] for w in range(windows)]

    def group_step(g):
        part_a, part_b = [], []
        for q in range(GROUP):
            p = g * GROUP + q
            real = half_a[p, head : head + WIN, :lanes]
            mean = jnp.sum(real, axis=0, keepdims=True) * (1.0 / WIN)
            real = real - jnp.where(zero_slot, mean, 0.0)
            part_a.append(jnp.concatenate([real, half_a[p, head : head + WIN, lanes:]], axis=1))
            lined = []
            for t in range(2):
                taken = half_b[t, p, pl.ds(offsets[0], SPAN), :]
                for w in range(1, windows):
                    taken = jnp.where(owner == w, half_b[t, p, pl.ds(offsets[w], SPAN), :], taken)
                lined.append(taken)
            part_b.append(jnp.concatenate(lined, axis=1))
        rows_a = jnp.concatenate(part_a, axis=0).astype(BF16)
        rows_b = jnp.concatenate(part_b, axis=0)
        high = rows_b.astype(BF16)
        low = (rows_b - high.astype(F32)).astype(BF16)
        spec_a = dot(left_ref[...], rows_a)
        spec_b = dot(rhigh_ref[...], high) + dot(rhigh_ref[...], low) + dot(rlow_ref[...], high)
        half_rows = GROUP * WIN
        a_cr, a_ci = spec_a[:half_rows, :lanes], spec_a[:half_rows, lanes:]
        a_sr, a_si = spec_a[half_rows:, :lanes], spec_a[half_rows:, lanes:]
        b_cr, b_ci = spec_b[:half_rows, :lanes], spec_b[:half_rows, lanes:]
        b_sr, b_si = spec_b[half_rows:, :lanes], spec_b[half_rows:, lanes:]
        b_cr = jnp.where(zero_slot & first_row, 0.0, b_cr)
        a_real, a_imag = a_cr + jnp.where(zero_slot, 0.0, a_si), jnp.where(zero_slot, 0.0, a_ci) - a_sr
        b_real, b_imag = b_cr + jnp.where(zero_slot, 0.0, b_si), jnp.where(zero_slot, 0.0, b_ci) - b_sr
        last_real = jnp.where(zero_slot, a_ci * b_ci + a_si * b_si, 0.0)
        last_imag = jnp.where(zero_slot, a_si * b_ci - a_ci * b_si, 0.0)
        cross_real = a_real * b_real + a_imag * b_imag - last_imag
        cross_imag = a_real * b_imag - a_imag * b_real + last_real
        for q in range(GROUP):
            b = phase_ref[g * GROUP + q]
            rows = slice(q * WIN, (q + 1) * WIN)
            sums[b, :, :lanes] += cross_real[rows]
            sums[b, :, lanes:] += cross_imag[rows]

    for g in range(pairs // GROUP):
        group_step(g)
    out_ref[...] = sums[...].astype(BF16)


def inverse_kernel(parts_ref, rows_ref, places_ref, out_ref, lines):
    windows = out_ref.shape[0]
    lanes = windows * SLOTS
    total = jnp.sum(parts_ref[...].astype(F32), axis=0)
    turned = dot(rows_ref[...], total, precision=HIGHEST)
    lines[:, :lanes] = turned[:WIN, :lanes] - turned[WIN:, lanes:]
    lines[:, lanes:] = turned[WIN:, :lanes] + turned[:WIN, lanes:]
    owner = (lax.broadcasted_iota(jnp.int32, (windows, 2 * lanes), 1) % lanes) // SLOTS
    own = owner == lax.broadcasted_iota(jnp.int32, (windows, 2 * lanes), 0)
    planes = None
    for r in range(4):
        spread = jnp.concatenate(
            [
                jnp.where(own, jnp.broadcast_to(lines[u : u + 1, :], (windows, 2 * lanes)), 0.0)
                for u in range(r, WIN, 4)
            ],
            axis=0,
        )
        term = dot(spread, places_ref[r], precision=HIGHEST)
        planes = term if planes is None else planes + term
    width = 4 * WIN
    for q in range(WIN // 4):
        out_ref[:, q * width : (q + 1) * width] = planes[q * windows : (q + 1) * windows]


def shifted(values, axis, step):
    count = lax.axis_size(axis)
    return lax.ppermute(values, axis, [(i, i + step) for i in range(count) if 0 <= i + step < count])


def call(kernel, outs, specs, scratch=(), flops=0, size=0):
    return pl.pallas_call(
        kernel,
        out_shape=outs,
        in_specs=specs,
        out_specs=jax.tree.map(lambda _: whole(), outs),
        scratch_shapes=scratch,
        cost_estimate=pl.CostEstimate(flops=flops, bytes_accessed=size, transcendentals=0),
    )


def body(frames, phase, shift, interp_rows, interp_cols):
    pairs, _, tile_rows, tile_cols = frames.shape
    windows = tile_cols // STEP
    lanes = windows * SLOTS
    bins = lax.axis_size("tm")
    fixed = constants(windows)
    shape = jax.ShapeDtypeStruct
    vmem, smem = whole(), whole(pltpu.SMEM)

    up = shifted(frames, "row", 1)
    down = shifted(frames, "row", -1)
    side = shape((HALO, 2 * pairs * tile_rows), BF16)
    rightward, leftward = call(strips_kernel, (side, side), [vmem], flops=10**7, size=200000)(frames)
    own_side = jnp.concatenate([shifted(rightward, "col", 1), shifted(leftward, "col", -1)], axis=0)
    up_side = shifted(own_side, "row", 1)
    down_side = shifted(own_side, "row", -1)

    wide = 2 * HALO + tile_cols
    high, low, rhigh, rlow = call(
        weights_kernel,
        (
            shape((wide, 2 * lanes), BF16),
            shape((wide, 2 * lanes), BF16),
            shape((2 * GROUP * WIN, GROUP * SPAN), BF16),
            shape((2 * GROUP * WIN, GROUP * SPAN), BF16),
        ),
        [smem] + [vmem] * 5,
        scratch=[pltpu.VMEM((2, wide + 8, lanes), F32)],
        flops=10**7,
        size=400000,
    )(shift, interp_rows, interp_cols, fixed["packed"], fixed["rows"], fixed["spread"])

    partial_sums = call(
        spectra_kernel,
        shape((bins, WIN, 2 * lanes), BF16),
        [smem, smem] + [vmem] * 12,
        scratch=[
            pltpu.VMEM((pairs, SPAN, 2 * lanes), F32),
            pltpu.VMEM((2, pairs, SPAN + 16, lanes), F32),
            pltpu.VMEM((bins, WIN, 2 * lanes), F32),
        ],
        flops=10**9,
        size=10**6,
    )(
        phase,
        shift,
        frames,
        up,
        down,
        own_side,
        up_side,
        down_side,
        fixed["first"],
        high,
        low,
        fixed["left_a"],
        rhigh,
        rlow,
    )
    parts = lax.all_to_all(partial_sums, "tm", 0, 0, tiled=True)
    planes = call(
        inverse_kernel,
        shape((windows, WIN * WIN), F32),
        [vmem] * 3,
        scratch=[pltpu.VMEM((WIN, 2 * lanes), F32)],
        flops=10**8,
        size=10**6,
    )(parts, fixed["inverse_rows"], fixed["places"])
    return planes[None, None]


def solution(mesh):
    placed = (P("tm", None, "row", "col"), P("tm"), P(None, "row", "col"), P(), P())
    return jax.shard_map(
        body, mesh=mesh, in_specs=placed, out_specs=P("tm", "row", "col", None), check_vma=False
    )
```

```python
import math
from functools import partial

import jax
import jax.numpy as jnp
import numpy as np
from jax import lax
from jax.experimental import pallas as pl
from jax.experimental.pallas import tpu as pltpu
from jax.sharding import PartitionSpec as P

WIN = 32
STEP = 16
BAND = 2
HALO = 16
SLOTS = WIN // 2
PATCH = WIN + 2 * BAND
SPAN = 48
GROUP = 4

F32 = jnp.float32
BF16 = jnp.bfloat16
HIGHEST = lax.Precision.HIGHEST


def dot(a, b, dims=((1,), (0,)), precision=None):
    return lax.dot_general(a, b, (dims, ((), ())), precision=precision, preferred_element_type=F32)


def tables():
    index = np.arange(WIN)
    angles = (index[:, None] * index[None, :] % WIN).astype(np.float32) * np.float32(2.0 * math.pi / WIN)
    return np.cos(angles).astype(np.float32), np.sin(angles).astype(np.float32)


def as_bf16(values):
    return np.asarray(values, np.float32).astype(jnp.bfloat16)


def constants(windows):
    cosine, sine = tables()
    cos_half = as_bf16(cosine).astype(np.float32)
    sin_half = as_bf16(sine).astype(np.float32)
    real = cos_half[:, :SLOTS]
    imag = -sin_half[:, :SLOTS]
    imag[:, 0] = cos_half[:, SLOTS]
    packed = np.concatenate([np.tile(real, (1, windows)), np.tile(imag, (1, windows))], axis=1)
    lanes = windows * SLOTS
    first = np.zeros((2 * HALO + windows * STEP, 2 * lanes), np.float32)
    for w in range(windows):
        top = HALO - (WIN - STEP) // 2 + STEP * w
        first[top : top + WIN, w * SLOTS : (w + 1) * SLOTS] = real
        first[top : top + WIN, lanes + w * SLOTS : lanes + (w + 1) * SLOTS] = imag
    rows = np.concatenate([np.tile(cos_half, (GROUP, 1)), np.tile(sin_half, (GROUP, 1))], axis=0)
    block = np.tile(np.repeat(np.arange(GROUP), WIN), 2)
    left_a = np.where(block[:, None] == np.repeat(np.arange(GROUP), WIN)[None, :], np.tile(rows, (1, GROUP)), 0.0)
    spread = np.zeros((PATCH, GROUP * SPAN), np.float32)
    for g in range(GROUP):
        spread[np.arange(PATCH), g * SPAN + np.arange(PATCH)] = 1.0
    lag = np.arange(WIN)
    back_real = 2.0 * cosine[:SLOTS]
    back_imag = -2.0 * sine[:SLOTS]
    back_real[0] = 1.0
    back_imag[0] = np.where(lag % 2 == 0, 1.0, -1.0)
    folded = np.concatenate([np.tile(back_real, (windows, 1)), np.tile(back_imag, (windows, 1))], axis=0) / WIN**3
    inverse_rows = np.concatenate([cosine, sine], axis=0)
    return dict(
        packed=as_bf16(packed),
        first=as_bf16(first),
        rows=as_bf16(rows),
        left_a=as_bf16(left_a),
        spread=as_bf16(spread),
        places=folded,
        inverse_rows=inverse_rows,
    )


def whole(space=pltpu.VMEM):
    return pl.BlockSpec(memory_space=space)


def strips_kernel(up_ref, own_ref, down_ref, right_ref, left_ref):
    pairs, _, tile_rows, tile_cols = own_ref.shape
    row = lax.broadcasted_iota(jnp.int32, (2 * HALO, tile_cols), 0)
    col = lax.broadcasted_iota(jnp.int32, (2 * HALO, tile_cols), 1)
    wanted = jnp.where(row < HALO, row + (tile_cols - HALO), row - HALO)
    pick = (col == wanted).astype(F32).astype(BF16)
    span = pairs * tile_rows
    for at, ref in enumerate((up_ref, own_ref, down_ref)):
        for image in range(2):
            pixels = ref[:, image].reshape(span, tile_cols)
            taken = dot(pick, pixels, ((1,), (1,))).astype(BF16)
            place = slice((2 * at + image) * span, (2 * at + image + 1) * span)
            right_ref[:, place] = taken[:HALO]
            left_ref[:, place] = taken[HALO:]


def weights_kernel(
    shift_ref, rows_ref, cols_ref, packed_ref, table_ref, spread_ref, high_ref, low_ref, rhigh_ref, rlow_ref, wide_ref
):
    windows = shift_ref.shape[2]
    lanes = wide_ref.shape[2]
    column = dot(cols_ref[...], packed_ref[...], ((0,), (0,)))
    column = jnp.concatenate([column, jnp.zeros((40 - PATCH, 2 * lanes), F32)], axis=0)
    wide_ref[...] = jnp.zeros_like(wide_ref)
    owner = lax.broadcasted_iota(jnp.int32, (40, lanes), 1) // SLOTS
    for w in range(windows):
        start = STEP * w + HALO - (WIN - STEP) // 2 - BAND + shift_ref[1, 0, w]
        rows = pl.ds(start, 40)
        for t in range(2):
            wide_ref[t, rows, :] = jnp.where(
                owner == w, column[:, t * lanes : (t + 1) * lanes], wide_ref[t, rows, :]
            )
    total = high_ref.shape[0]
    values = jnp.concatenate([wide_ref[0, :total, :], wide_ref[1, :total, :]], axis=1)
    high = values.astype(BF16)
    high_ref[...] = high
    low_ref[...] = (values - high.astype(F32)).astype(BF16)
    spread = dot(rows_ref[...], spread_ref[...]).astype(BF16)
    left = dot(table_ref[...], spread)
    mine = (lax.broadcasted_iota(jnp.int32, left.shape, 0) // WIN) % GROUP
    theirs = lax.broadcasted_iota(jnp.int32, left.shape, 1) // SPAN
    left = jnp.where(mine == theirs, left, 0.0)
    high = left.astype(BF16)
    rhigh_ref[...] = high
    rlow_ref[...] = (left - high.astype(F32)).astype(BF16)


def spectra_kernel(
    phase_ref,
    shift_ref,
    own_ref,
    up_ref,
    down_ref,
    before_ref,
    after_ref,
    first_ref,
    high_ref,
    low_ref,
    left_ref,
    rhigh_ref,
    rlow_ref,
    out_ref,
    half_a,
    half_b,
    sums,
):
    pairs, _, tile_rows, tile_cols = own_ref.shape
    windows = shift_ref.shape[2]
    lanes = windows * SLOTS
    span = pairs * tile_rows
    right = HALO + tile_cols

    def along_columns(pixels, strip, weights):
        edge = jnp.concatenate([weights[:HALO], weights[right:]], axis=0)
        return dot(pixels, weights[HALO:right]) + dot(strip, edge)

    for at, ref in enumerate((up_ref, own_ref, down_ref)):
        rows = slice(at * tile_rows, (at + 1) * tile_rows)
        strips = []
        for image in range(2):
            place = slice((2 * at + image) * span, (2 * at + image + 1) * span)
            strip = jnp.concatenate([before_ref[:, place], after_ref[:, place]], axis=0)
            strips.append(jnp.transpose(strip.astype(F32)).astype(BF16))
        pixels = ref[:, 0].reshape(span, tile_cols)
        half = along_columns(pixels, strips[0], first_ref[...])
        half_a[:, rows, :] = half.reshape(pairs, tile_rows, 2 * lanes)
        pixels = ref[:, 1].reshape(span, tile_cols)
        half = along_columns(pixels, strips[1], high_ref[...]) + along_columns(pixels, strips[1], low_ref[...])
        for t in range(2):
            half_b[t, :, rows, :] = half[:, t * lanes : (t + 1) * lanes].reshape(pairs, tile_rows, lanes)
    half_b[:, :, 3 * tile_rows :, :] = jnp.zeros((2, pairs, half_b.shape[2] - 3 * tile_rows, lanes), F32)
    sums[...] = jnp.zeros_like(sums)

    head = tile_rows - (WIN - STEP) // 2
    zero_slot = lax.broadcasted_iota(jnp.int32, (1, lanes), 1) % SLOTS == 0
    owner = lax.broadcasted_iota(jnp.int32, (1, lanes), 1) // SLOTS
    first_row = lax.broadcasted_iota(jnp.int32, (GROUP * WIN, 1), 0) % WIN == 0
    offsets = [HALO - (WIN - STEP) // 2 - BAND + shift_ref[0, 0, w] for w in range(windows)]

    def group_step(g):
        part_a, part_b = [], []
        for q in range(GROUP):
            p = g * GROUP + q
            real = half_a[p, head : head + WIN, :lanes]
            mean = jnp.sum(real, axis=0, keepdims=True) * (1.0 / WIN)
            real = real - jnp.where(zero_slot, mean, 0.0)
            part_a.append(jnp.concatenate([real, half_a[p, head : head + WIN, lanes:]], axis=1))
            lined = []
            for t in range(2):
                taken = half_b[t, p, pl.ds(offsets[0], SPAN), :]
                for w in range(1, windows):
                    taken = jnp.where(owner == w, half_b[t, p, pl.ds(offsets[w], SPAN), :], taken)
                lined.append(taken)
            part_b.append(jnp.concatenate(lined, axis=1))
        rows_a = jnp.concatenate(part_a, axis=0).astype(BF16)
        rows_b = jnp.concatenate(part_b, axis=0)
        high = rows_b.astype(BF16)
        low = (rows_b - high.astype(F32)).astype(BF16)
        spec_a = dot(left_ref[...], rows_a)
        spec_b = dot(rhigh_ref[...], high) + dot(rhigh_ref[...], low) + dot(rlow_ref[...], high)
        half_rows = GROUP * WIN
        a_cr, a_ci = spec_a[:half_rows, :lanes], spec_a[:half_rows, lanes:]
        a_sr, a_si = spec_a[half_rows:, :lanes], spec_a[half_rows:, lanes:]
        b_cr, b_ci = spec_b[:half_rows, :lanes], spec_b[:half_rows, lanes:]
        b_sr, b_si = spec_b[half_rows:, :lanes], spec_b[half_rows:, lanes:]
        b_cr = jnp.where(zero_slot & first_row, 0.0, b_cr)
        a_real, a_imag = a_cr + jnp.where(zero_slot, 0.0, a_si), jnp.where(zero_slot, 0.0, a_ci) - a_sr
        b_real, b_imag = b_cr + jnp.where(zero_slot, 0.0, b_si), jnp.where(zero_slot, 0.0, b_ci) - b_sr
        last_real = jnp.where(zero_slot, a_ci * b_ci + a_si * b_si, 0.0)
        last_imag = jnp.where(zero_slot, a_si * b_ci - a_ci * b_si, 0.0)
        cross_real = a_real * b_real + a_imag * b_imag - last_imag
        cross_imag = a_real * b_imag - a_imag * b_real + last_real
        for q in range(GROUP):
            b = phase_ref[g * GROUP + q]
            rows = slice(q * WIN, (q + 1) * WIN)
            sums[b, :, :lanes] += cross_real[rows]
            sums[b, :, lanes:] += cross_imag[rows]

    for g in range(pairs // GROUP):
        group_step(g)
    out_ref[...] = sums[...].astype(BF16)


def inverse_kernel(parts_ref, rows_ref, places_ref, out_ref, lines):
    windows = out_ref.shape[0]
    lanes = windows * SLOTS
    total = jnp.sum(parts_ref[...].astype(F32), axis=0)
    turned = dot(rows_ref[...], total, precision=HIGHEST)
    lines[:, :lanes] = turned[:WIN, :lanes] - turned[WIN:, lanes:]
    lines[:, lanes:] = turned[WIN:, :lanes] + turned[:WIN, lanes:]
    owner = (lax.broadcasted_iota(jnp.int32, (windows, 2 * lanes), 1) % lanes) // SLOTS
    own = owner == lax.broadcasted_iota(jnp.int32, (windows, 2 * lanes), 0)
    spread = jnp.concatenate(
        [jnp.where(own, jnp.broadcast_to(lines[u : u + 1, :], (windows, 2 * lanes)), 0.0) for u in range(WIN)],
        axis=0,
    )
    planes = dot(spread, places_ref[...], precision=HIGHEST)
    for u in range(WIN):
        out_ref[:, u * WIN : (u + 1) * WIN] = planes[u * windows : (u + 1) * windows]


def shifted(values, axis, step):
    count = lax.axis_size(axis)
    return lax.ppermute(values, axis, [(i, i + step) for i in range(count) if 0 <= i + step < count])


def call(kernel, outs, specs, scratch=(), flops=0, size=0, room=16):
    return pl.pallas_call(
        kernel,
        out_shape=outs,
        in_specs=specs,
        out_specs=jax.tree.map(lambda _: whole(), outs),
        scratch_shapes=scratch,
        compiler_params=pltpu.CompilerParams(vmem_limit_bytes=room << 20),
        cost_estimate=pl.CostEstimate(flops=flops, bytes_accessed=size, transcendentals=0),
    )


def body(frames, phase, shift, interp_rows, interp_cols):
    pairs, _, tile_rows, tile_cols = frames.shape
    windows = tile_cols // STEP
    lanes = windows * SLOTS
    bins = lax.axis_size("tm")
    fixed = constants(windows)
    shape = jax.ShapeDtypeStruct
    vmem, smem = whole(), whole(pltpu.SMEM)

    up = shifted(frames, "row", 1)
    down = shifted(frames, "row", -1)
    side = shape((HALO, 6 * pairs * tile_rows), BF16)
    rightward, leftward = call(strips_kernel, (side, side), [vmem] * 3, flops=10**7, size=200000)(up, frames, down)
    before = shifted(rightward, "col", 1)
    after = shifted(leftward, "col", -1)

    wide = 2 * HALO + tile_cols
    high, low, rhigh, rlow = call(
        weights_kernel,
        (
            shape((wide, 2 * lanes), BF16),
            shape((wide, 2 * lanes), BF16),
            shape((2 * GROUP * WIN, GROUP * SPAN), BF16),
            shape((2 * GROUP * WIN, GROUP * SPAN), BF16),
        ),
        [smem] + [vmem] * 5,
        scratch=[pltpu.VMEM((2, wide + 8, lanes), F32)],
        flops=10**7,
        size=400000,
    )(shift, interp_rows, interp_cols, fixed["packed"], fixed["rows"], fixed["spread"])

    partial_sums = call(
        spectra_kernel,
        shape((bins, WIN, 2 * lanes), BF16),
        [smem, smem] + [vmem] * 11,
        scratch=[
            pltpu.VMEM((pairs, SPAN, 2 * lanes), F32),
            pltpu.VMEM((2, pairs, SPAN + 16, lanes), F32),
            pltpu.VMEM((bins, WIN, 2 * lanes), F32),
        ],
        flops=10**9,
        size=10**6,
    )(
        phase,
        shift,
        frames,
        up,
        down,
        before,
        after,
        fixed["first"],
        high,
        low,
        fixed["left_a"],
        rhigh,
        rlow,
    )
    parts = lax.all_to_all(partial_sums, "tm", 0, 0, tiled=True)
    planes = call(
        inverse_kernel,
        shape((windows, WIN * WIN), F32),
        [vmem] * 3,
        scratch=[pltpu.VMEM((WIN, 2 * lanes), F32)],
        flops=10**8,
        size=10**6,
    )(parts, fixed["inverse_rows"], fixed["places"])
    return planes[None, None]


def solution(mesh):
    placed = (P("tm", None, "row", "col"), P("tm"), P(None, "row", "col"), P(), P())
    return jax.shard_map(
        body, mesh=mesh, in_specs=placed, out_specs=P("tm", "row", "col", None), check_vma=False
    )
```

```python
import math
from functools import partial

import jax
import jax.numpy as jnp
import numpy as np
from jax import lax
from jax.experimental import pallas as pl
from jax.experimental.pallas import tpu as pltpu
from jax.sharding import PartitionSpec as P

WIN = 32
STEP = 16
BAND = 2
HALO = 16
SLOTS = WIN // 2
PATCH = WIN + 2 * BAND
SPAN = 40
GROUP = 4
QUARTERS = 4

F32 = jnp.float32
BF16 = jnp.bfloat16
HIGHEST = lax.Precision.HIGHEST


def dot(a, b, dims=((1,), (0,)), precision=None):
    return lax.dot_general(a, b, (dims, ((), ())), precision=precision, preferred_element_type=F32)


def tables():
    index = np.arange(WIN)
    angles = (index[:, None] * index[None, :] % WIN).astype(np.float32) * np.float32(2.0 * math.pi / WIN)
    return np.cos(angles).astype(np.float32), np.sin(angles).astype(np.float32)


def as_bf16(values):
    return np.asarray(values, np.float32).astype(jnp.bfloat16)


def constants(windows):
    cosine, sine = tables()
    cos_half = as_bf16(cosine).astype(np.float32)
    sin_half = as_bf16(sine).astype(np.float32)
    real = cos_half[:, :SLOTS]
    imag = -sin_half[:, :SLOTS]
    imag[:, 0] = cos_half[:, SLOTS]
    packed = np.concatenate([np.tile(real, (1, windows)), np.tile(imag, (1, windows))], axis=1)
    lanes = windows * SLOTS
    first = np.zeros((2 * HALO + windows * STEP, 2 * lanes), np.float32)
    for w in range(windows):
        top = HALO - (WIN - STEP) // 2 + STEP * w
        first[top : top + WIN, w * SLOTS : (w + 1) * SLOTS] = real
        first[top : top + WIN, lanes + w * SLOTS : lanes + (w + 1) * SLOTS] = imag
    own = first[HALO : HALO + windows * STEP]
    order = np.concatenate([own, first[:HALO], first[HALO + windows * STEP :]], axis=0)
    edges = np.zeros((QUARTERS,) + order.shape, np.float32)
    for h in range(QUARTERS):
        for half in range(2):
            for at, w in enumerate((0, windows - 1)):
                to = half * lanes + (2 * h + at) * SLOTS
                of = half * lanes + w * SLOTS
                edges[h, :, to : to + SLOTS] = order[:, of : of + SLOTS]
    rows = np.concatenate([np.tile(cos_half, (GROUP, 1)), np.tile(sin_half, (GROUP, 1))], axis=0)
    block = np.tile(np.repeat(np.arange(GROUP), WIN), 2)
    left_a = np.where(block[:, None] == np.repeat(np.arange(GROUP), WIN)[None, :], np.tile(rows, (1, GROUP)), 0.0)
    lag = np.arange(WIN)
    back_real = 2.0 * cosine[:SLOTS]
    back_imag = -2.0 * sine[:SLOTS]
    back_real[0] = 1.0
    back_imag[0] = np.where(lag % 2 == 0, 1.0, -1.0)
    folded = np.concatenate([np.tile(back_real, (windows, 1)), np.tile(back_imag, (windows, 1))], axis=0) / WIN**3
    inverse_rows = np.concatenate([cosine, sine], axis=0)
    return dict(
        table=as_bf16(np.concatenate([packed, rows.T], axis=1)),
        own=as_bf16(own),
        edges=as_bf16(edges),
        left_a=as_bf16(left_a),
        places=folded,
        inverse_rows=inverse_rows,
    )


def whole(space=pltpu.VMEM):
    return pl.BlockSpec(memory_space=space)


def take_strips(ref, right_ref, left_ref, start):
    pairs, _, tile_rows, tile_cols = ref.shape
    row = lax.broadcasted_iota(jnp.int32, (2 * HALO, tile_cols), 0)
    col = lax.broadcasted_iota(jnp.int32, (2 * HALO, tile_cols), 1)
    wanted = jnp.where(row < HALO, row + (tile_cols - HALO), row - HALO)
    pick = (col == wanted).astype(F32).astype(BF16)
    span = pairs * tile_rows
    for image in range(2):
        pixels = ref[:, image].reshape(span, tile_cols)
        taken = dot(pick, pixels, ((1,), (1,))).astype(BF16)
        place = slice(start + image * span, start + (image + 1) * span)
        right_ref[:, place] = taken[:HALO]
        left_ref[:, place] = taken[HALO:]


def strips_kernel(up_ref, own_right_ref, own_left_ref, down_ref, right_ref, left_ref):
    width = own_right_ref.shape[1]
    take_strips(up_ref, right_ref, left_ref, 0)
    right_ref[:, width : 2 * width] = own_right_ref[...]
    left_ref[:, width : 2 * width] = own_left_ref[...]
    take_strips(down_ref, right_ref, left_ref, 2 * width)


def fetch(sources, targets, sems):
    copies = [pltpu.make_async_copy(a, b, sems.at[i]) for i, (a, b) in enumerate(zip(sources, targets))]
    for copy in copies:
        copy.start()
    return copies


def weights_kernel(
    shift_hbm,
    phase_hbm,
    frames_hbm,
    rows_hbm,
    cols_hbm,
    table_hbm,
    moved_ref,
    bins_ref,
    own_ref,
    high_ref,
    low_ref,
    ehigh_ref,
    elow_ref,
    rhigh_ref,
    rlow_ref,
    right_ref,
    left_ref,
    shift_ref,
    rows_ref,
    cols_ref,
    table_ref,
    wide_ref,
    sems,
):
    copies = fetch(
        (shift_hbm, rows_hbm, cols_hbm, table_hbm, shift_hbm, phase_hbm, frames_hbm),
        (shift_ref, rows_ref, cols_ref, table_ref, moved_ref, bins_ref, own_ref),
        sems,
    )
    windows = shift_ref.shape[2]
    lanes = wide_ref.shape[2]
    for copy in copies[:4]:
        copy.wait()
    packed, turned = table_ref[:, : 2 * lanes], table_ref[:, 2 * lanes :]
    column = dot(cols_ref[...], packed, ((0,), (0,)))
    column = jnp.concatenate([column, jnp.zeros((40 - PATCH, 2 * lanes), F32)], axis=0)
    wide_ref[...] = jnp.zeros_like(wide_ref)
    owner = lax.broadcasted_iota(jnp.int32, (40, lanes), 1) // SLOTS
    for w in range(windows):
        start = STEP * w + HALO - (WIN - STEP) // 2 - BAND + shift_ref[1, 0, w]
        rows = pl.ds(start, 40)
        for t in range(2):
            wide_ref[t, rows, :] = jnp.where(
                owner == w, column[:, t * lanes : (t + 1) * lanes], wide_ref[t, rows, :]
            )
    inner = slice(HALO, HALO + high_ref.shape[0])
    right = slice(inner.stop, inner.stop + HALO)
    lane = lax.broadcasted_iota(jnp.int32, (1, lanes), 1)
    for t in range(2):
        place = slice(t * lanes, (t + 1) * lanes)
        values = wide_ref[t, inner, :]
        high = values.astype(BF16)
        high_ref[:, place] = high
        low_ref[:, place] = (values - high.astype(F32)).astype(BF16)
        values = jnp.concatenate([values, wide_ref[t, :HALO, :], wide_ref[t, right, :]], axis=0)
        ends = jnp.where(lane < SLOTS, values, 0.0) + jnp.where(
            lane // SLOTS == 1, pltpu.roll(values, 2 * SLOTS, 1), 0.0
        )
        for h in range(QUARTERS):
            placed = ends if h == 0 else pltpu.roll(ends, 2 * SLOTS * h, 1)
            high = placed.astype(BF16)
            ehigh_ref[h, :, place] = high
            elow_ref[h, :, place] = (placed - high.astype(F32)).astype(BF16)
    place = lax.broadcasted_iota(jnp.int32, (PATCH, GROUP * SPAN), 1) % SPAN
    spread = (place == lax.broadcasted_iota(jnp.int32, (PATCH, GROUP * SPAN), 0)).astype(F32).astype(BF16)
    spread = dot(rows_ref[...], spread).astype(BF16)
    left = dot(turned, spread, ((0,), (0,)))
    mine = (lax.broadcasted_iota(jnp.int32, left.shape, 0) // WIN) % GROUP
    theirs = lax.broadcasted_iota(jnp.int32, left.shape, 1) // SPAN
    left = jnp.where(mine == theirs, left, 0.0)
    high = left.astype(BF16)
    rhigh_ref[...] = high
    rlow_ref[...] = (left - high.astype(F32)).astype(BF16)
    for copy in copies[4:]:
        copy.wait()
    take_strips(own_ref, right_ref, left_ref, 0)


def starts(shift_ref, windows):
    return [HALO - (WIN - STEP) // 2 - BAND + shift_ref[0, 0, w] for w in windows]


def cross_spectra(half_a, half_b, pairs, offsets, owner, left_ref, rhigh_ref, rlow_ref):
    lanes = half_b.shape[3]
    head = (half_a.shape[1] - WIN) // 2
    zero_slot = lax.broadcasted_iota(jnp.int32, (1, lanes), 1) % SLOTS == 0
    first_row = lax.broadcasted_iota(jnp.int32, (GROUP * WIN, 1), 0) % WIN == 0
    part_a, part_b = [], []
    for p in pairs:
        real = half_a[p, head : head + WIN, :lanes]
        mean = jnp.sum(real, axis=0, keepdims=True) * (1.0 / WIN)
        real = real - jnp.where(zero_slot, mean, 0.0)
        part_a.append(jnp.concatenate([real, half_a[p, head : head + WIN, lanes:]], axis=1))
        lined = []
        for t in range(2):
            taken = half_b[t, p, pl.ds(offsets[0], SPAN), :]
            for w in range(1, len(offsets)):
                taken = jnp.where(owner == w, half_b[t, p, pl.ds(offsets[w], SPAN), :], taken)
            lined.append(taken)
        part_b.append(jnp.concatenate(lined, axis=1))
    rows_a = jnp.concatenate(part_a, axis=0).astype(BF16)
    rows_b = jnp.concatenate(part_b, axis=0)
    high = rows_b.astype(BF16)
    low = (rows_b - high.astype(F32)).astype(BF16)
    spec_a = dot(left_ref[...], rows_a)
    spec_b = dot(rhigh_ref[...], high) + dot(rhigh_ref[...], low) + dot(rlow_ref[...], high)
    half_rows = GROUP * WIN
    a_cr, a_ci = spec_a[:half_rows, :lanes], spec_a[:half_rows, lanes:]
    a_sr, a_si = spec_a[half_rows:, :lanes], spec_a[half_rows:, lanes:]
    b_cr, b_ci = spec_b[:half_rows, :lanes], spec_b[:half_rows, lanes:]
    b_sr, b_si = spec_b[half_rows:, :lanes], spec_b[half_rows:, lanes:]
    b_cr = jnp.where(zero_slot & first_row, 0.0, b_cr)
    a_real, a_imag = a_cr + jnp.where(zero_slot, 0.0, a_si), jnp.where(zero_slot, 0.0, a_ci) - a_sr
    b_real, b_imag = b_cr + jnp.where(zero_slot, 0.0, b_si), jnp.where(zero_slot, 0.0, b_ci) - b_sr
    last_real = jnp.where(zero_slot, a_ci * b_ci + a_si * b_si, 0.0)
    last_imag = jnp.where(zero_slot, a_si * b_ci - a_ci * b_si, 0.0)
    cross_real = a_real * b_real + a_imag * b_imag - last_imag
    cross_imag = a_real * b_imag - a_imag * b_real + last_real
    return cross_real, cross_imag


def inner_kernel(
    phase_vec,
    shift_vec,
    own_ref,
    up_ref,
    down_ref,
    first_ref,
    high_ref,
    low_ref,
    left_ref,
    rhigh_ref,
    rlow_ref,
    sums,
    half_a,
    half_b,
    phase_ref,
    shift_ref,
    sems,
):
    copies = fetch((phase_vec, shift_vec), (phase_ref, shift_ref), sems)
    pairs, _, tile_rows, tile_cols = own_ref.shape
    windows = shift_ref.shape[2]
    lanes = windows * SLOTS
    span = pairs * tile_rows
    for at, ref in enumerate((up_ref, own_ref, down_ref)):
        rows = slice(at * tile_rows, (at + 1) * tile_rows)
        pixels = ref[:, 0].reshape(span, tile_cols)
        half_a[:, rows, :] = dot(pixels, first_ref[...]).reshape(pairs, tile_rows, 2 * lanes)
        pixels = ref[:, 1].reshape(span, tile_cols)
        half = dot(pixels, high_ref[...]) + dot(pixels, low_ref[...])
        for t in range(2):
            half_b[t, :, rows, :] = half[:, t * lanes : (t + 1) * lanes].reshape(pairs, tile_rows, lanes)
    half_b[:, :, 3 * tile_rows :, :] = jnp.zeros((2, pairs, half_b.shape[2] - 3 * tile_rows, lanes), F32)
    sums[...] = jnp.zeros_like(sums)
    owner = lax.broadcasted_iota(jnp.int32, (1, lanes), 1) // SLOTS
    for copy in copies:
        copy.wait()
    offsets = starts(shift_ref, range(windows))
    for g in range(pairs // GROUP):
        members = range(g * GROUP, (g + 1) * GROUP)
        real, imag = cross_spectra(half_a, half_b, members, offsets, owner, left_ref, rhigh_ref, rlow_ref)
        for q, p in enumerate(members):
            b = phase_ref[p]
            rows = slice(q * WIN, (q + 1) * WIN)
            sums[b, :, :lanes] += real[rows]
            sums[b, :, lanes:] += imag[rows]


def edge_kernel(
    phase_vec,
    shift_vec,
    own_ref,
    up_ref,
    down_ref,
    before_ref,
    after_ref,
    first_ref,
    high_ref,
    low_ref,
    left_ref,
    rhigh_ref,
    rlow_ref,
    inner_ref,
    out_ref,
    half_a,
    half_b,
    sums,
    phase_ref,
    shift_ref,
    sems,
):
    copies = fetch((phase_vec, shift_vec), (phase_ref, shift_ref), sems)
    pairs, _, tile_rows, tile_cols = own_ref.shape
    windows = shift_ref.shape[2]
    lanes = windows * SLOTS
    span = pairs * tile_rows
    part = span // QUARTERS
    each = pairs // QUARTERS

    def along_columns(pixels, weights_ref):
        total = dot(pixels[:part], weights_ref[0])
        for h in range(1, QUARTERS):
            total = total + dot(pixels[h * part : (h + 1) * part], weights_ref[h])
        return total

    for at, ref in enumerate((up_ref, own_ref, down_ref)):
        rows = slice(at * tile_rows, (at + 1) * tile_rows)
        taken = []
        for image in range(2):
            place = slice((2 * at + image) * span, (2 * at + image + 1) * span)
            strip = jnp.concatenate([before_ref[:, place], after_ref[:, place]], axis=0)
            strip = jnp.transpose(strip.astype(F32)).astype(BF16)
            taken.append(jnp.concatenate([ref[:, image].reshape(span, tile_cols), strip], axis=1))
        half_a[:, rows, :] = along_columns(taken[0], first_ref).reshape(each, tile_rows, 2 * lanes)
        half = along_columns(taken[1], high_ref) + along_columns(taken[1], low_ref)
        for t in range(2):
            half_b[t, :, rows, :] = half[:, t * lanes : (t + 1) * lanes].reshape(each, tile_rows, lanes)
    half_b[:, :, 3 * tile_rows :, :] = jnp.zeros((2, each, half_b.shape[2] - 3 * tile_rows, lanes), F32)
    sums[...] = jnp.zeros_like(sums)
    lane = lax.broadcasted_iota(jnp.int32, (1, lanes), 1)
    for copy in copies:
        copy.wait()
    offsets = starts(shift_ref, (0, windows - 1))
    real, imag = cross_spectra(
        half_a, half_b, range(each), offsets, (lane // SLOTS) % 2, left_ref, rhigh_ref, rlow_ref
    )
    for q in range(each):
        rows = slice(q * WIN, (q + 1) * WIN)
        for h in range(QUARTERS):
            b = phase_ref[h * each + q]
            mine = lane // (2 * SLOTS) == h
            sums[b, :, :lanes] += jnp.where(mine, real[rows], 0.0)
            sums[b, :, lanes:] += jnp.where(mine, imag[rows], 0.0)
    edge = (lane < SLOTS) | (lane >= lanes - SLOTS)
    for b in range(sums.shape[0]):
        for t in range(2):
            place = slice(t * lanes, (t + 1) * lanes)
            total = sums[b, :, place]
            total = total + pltpu.roll(total, lanes // 2, 1)
            total = total + pltpu.roll(total, lanes // 4, 1)
            out_ref[b, :, place] = jnp.where(edge, total, inner_ref[b, :, place]).astype(BF16)


def inverse_kernel(parts_ref, rows_ref, places_ref, out_ref, lines):
    windows = out_ref.shape[0]
    lanes = windows * SLOTS
    total = jnp.sum(parts_ref[...].astype(F32), axis=0)
    turned = dot(rows_ref[...], total, precision=HIGHEST)
    lines[:, :lanes] = turned[:WIN, :lanes] - turned[WIN:, lanes:]
    lines[:, lanes:] = turned[WIN:, :lanes] + turned[:WIN, lanes:]
    owner = (lax.broadcasted_iota(jnp.int32, (windows, 2 * lanes), 1) % lanes) // SLOTS
    own = owner == lax.broadcasted_iota(jnp.int32, (windows, 2 * lanes), 0)
    spread = jnp.concatenate(
        [jnp.where(own, jnp.broadcast_to(lines[u : u + 1, :], (windows, 2 * lanes)), 0.0) for u in range(WIN)],
        axis=0,
    )
    planes = dot(spread, places_ref[...], precision=HIGHEST)
    for u in range(WIN):
        out_ref[:, u * WIN : (u + 1) * WIN] = planes[u * windows : (u + 1) * windows]


def shifted(values, axis, step):
    count = lax.axis_size(axis)
    return lax.ppermute(values, axis, [(i, i + step) for i in range(count) if 0 <= i + step < count])


def stay(*values):
    return [pltpu.with_memory_space_constraint(jnp.asarray(value), pltpu.HBM) for value in values]


def call(kernel, outs, specs, scratch=(), flops=0, size=0, room=16):
    return pl.pallas_call(
        kernel,
        out_shape=outs,
        in_specs=specs,
        out_specs=jax.tree.map(lambda _: whole(), outs),
        scratch_shapes=scratch,
        compiler_params=pltpu.CompilerParams(vmem_limit_bytes=room << 20),
        cost_estimate=pl.CostEstimate(flops=flops, bytes_accessed=size, transcendentals=0),
    )


def body(frames, phase, shift, interp_rows, interp_cols):
    pairs, _, tile_rows, tile_cols = frames.shape
    windows = tile_cols // STEP
    lanes = windows * SLOTS
    bins = lax.axis_size("tm")
    fixed = constants(windows)
    shape = jax.ShapeDtypeStruct
    vmem, hbm = whole(), whole(pltpu.HBM)

    up = shifted(frames, "row", 1)
    down = shifted(frames, "row", -1)
    wide = 2 * HALO + tile_cols
    strip = shape((HALO, 2 * pairs * tile_rows), BF16)
    scalars = pltpu.SMEM(shift.shape, shift.dtype)
    weights = shape((tile_cols, 2 * lanes), BF16)
    ends = shape((QUARTERS, wide, 2 * lanes), BF16)
    left = shape((2 * GROUP * WIN, GROUP * SPAN), BF16)
    moved, phases, own, high, low, ehigh, elow, rhigh, rlow, own_right, own_left = call(
        weights_kernel,
        (
            shape(shift.shape, shift.dtype),
            shape(phase.shape, phase.dtype),
            shape(frames.shape, BF16),
            weights,
            weights,
            ends,
            ends,
            left,
            left,
            strip,
            strip,
        ),
        [hbm] * 6,
        scratch=[
            scalars,
            pltpu.VMEM(interp_rows.shape, BF16),
            pltpu.VMEM(interp_cols.shape, BF16),
            pltpu.VMEM(fixed["table"].shape, BF16),
            pltpu.VMEM((2, wide + 8, lanes), F32),
            pltpu.SemaphoreType.DMA((7,)),
        ],
        flops=10**7,
        size=400000,
    )(*stay(shift, phase, frames, interp_rows, interp_cols, fixed["table"]))

    side = shape((HALO, 6 * pairs * tile_rows), BF16)
    rightward, leftward = call(strips_kernel, (side, side), [vmem] * 4, flops=10**7, size=200000)(
        up, own_right, own_left, down
    )
    before = shifted(rightward, "col", 1)
    after = shifted(leftward, "col", -1)

    tall = 3 * tile_rows
    fetched = [pltpu.SMEM(phase.shape, phase.dtype), scalars, pltpu.SemaphoreType.DMA((2,))]
    inner = call(
        inner_kernel,
        shape((bins, WIN, 2 * lanes), F32),
        [vmem] * 11,
        scratch=[pltpu.VMEM((pairs, tall, 2 * lanes), F32), pltpu.VMEM((2, pairs, tall + 8, lanes), F32)] + fetched,
        flops=10**9,
        size=10**6,
    )(phases, moved, own, up, down, fixed["own"], high, low, fixed["left_a"], rhigh, rlow)
    each = pairs // QUARTERS
    partial_sums = call(
        edge_kernel,
        shape((bins, WIN, 2 * lanes), BF16),
        [vmem] * 14,
        scratch=[
            pltpu.VMEM((each, tall, 2 * lanes), F32),
            pltpu.VMEM((2, each, tall + 8, lanes), F32),
            pltpu.VMEM((bins, WIN, 2 * lanes), F32),
        ]
        + fetched,
        flops=10**9,
        size=10**6,
    )(
        phases,
        moved,
        own,
        up,
        down,
        before,
        after,
        fixed["edges"],
        ehigh,
        elow,
        fixed["left_a"],
        rhigh,
        rlow,
        inner,
    )
    parts = lax.all_to_all(partial_sums, "tm", 0, 0, tiled=True)
    planes = call(
        inverse_kernel,
        shape((windows, WIN * WIN), F32),
        [vmem] * 3,
        scratch=[pltpu.VMEM((WIN, 2 * lanes), F32)],
        flops=10**8,
        size=10**6,
    )(parts, fixed["inverse_rows"], fixed["places"])
    return planes[None, None]


def solution(mesh):
    placed = (P("tm", None, "row", "col"), P("tm"), P(None, "row", "col"), P(), P())
    return jax.shard_map(
        body, mesh=mesh, in_specs=placed, out_specs=P("tm", "row", "col", None), check_vma=False
    )
```

```python
import math

import jax
import jax.numpy as jnp
import numpy as np
from jax import lax
from jax.experimental import pallas as pl
from jax.experimental.pallas import tpu as pltpu
from jax.sharding import PartitionSpec as P


WIN = 32
STEP = 16
BAND = 2
HALO = 16
SLOTS = WIN // 2
PATCH = WIN + 2 * BAND
SPAN = 40
GROUP = 4
QUARTERS = 4

F32 = jnp.float32
BF16 = jnp.bfloat16


def dot(a, b, dims=((1,), (0,))):
    return lax.dot_general(a, b, (dims, ((), ())), preferred_element_type=F32)


def tables():
    index = np.arange(WIN)
    angles = (index[:, None] * index[None, :] % WIN).astype(np.float32) * np.float32(2.0 * math.pi / WIN)
    return np.cos(angles).astype(np.float32), np.sin(angles).astype(np.float32)


def as_bf16(values):
    return np.asarray(values, np.float32).astype(jnp.bfloat16)


def constants(windows):
    cosine, sine = tables()
    cos_half = as_bf16(cosine).astype(np.float32)
    sin_half = as_bf16(sine).astype(np.float32)
    real = cos_half[:, :SLOTS]
    imag = -sin_half[:, :SLOTS]
    imag[:, 0] = cos_half[:, SLOTS]
    packed = np.concatenate([np.tile(real, (1, windows)), np.tile(imag, (1, windows))], axis=1)
    lanes = windows * SLOTS
    first = np.zeros((2 * HALO + windows * STEP, 2 * lanes), np.float32)
    for w in range(windows):
        top = HALO - (WIN - STEP) // 2 + STEP * w
        first[top : top + WIN, w * SLOTS : (w + 1) * SLOTS] = real
        first[top : top + WIN, lanes + w * SLOTS : lanes + (w + 1) * SLOTS] = imag
    own = first[HALO : HALO + windows * STEP]
    order = np.concatenate([own, first[:HALO], first[HALO + windows * STEP :]], axis=0)
    edges = np.zeros((QUARTERS,) + order.shape, np.float32)
    for h in range(QUARTERS):
        for half in range(2):
            for at, w in enumerate((0, windows - 1)):
                to = half * lanes + (2 * h + at) * SLOTS
                of = half * lanes + w * SLOTS
                edges[h, :, to : to + SLOTS] = order[:, of : of + SLOTS]
    rows = np.concatenate([np.tile(cos_half, (GROUP, 1)), np.tile(sin_half, (GROUP, 1))], axis=0)
    block = np.tile(np.repeat(np.arange(GROUP), WIN), 2)
    left_a = np.where(block[:, None] == np.repeat(np.arange(GROUP), WIN)[None, :], np.tile(rows, (1, GROUP)), 0.0)
    lag = np.arange(WIN)
    back_real = 2.0 * cosine[:SLOTS]
    back_imag = -2.0 * sine[:SLOTS]
    back_real[0] = 1.0
    back_imag[0] = np.where(lag % 2 == 0, 1.0, -1.0)
    folded = np.concatenate([np.tile(back_real, (windows, 1)), np.tile(back_imag, (windows, 1))], axis=0) / WIN**3
    inverse_rows = np.concatenate([cosine, sine], axis=0)
    return dict(
        table=as_bf16(np.concatenate([packed, rows.T], axis=1)),
        own=as_bf16(own),
        edges=as_bf16(edges),
        left_a=as_bf16(left_a),
        places=folded,
        inverse_rows=inverse_rows,
    )


def whole(space=pltpu.VMEM):
    return pl.BlockSpec(memory_space=space)


def take_strips(ref, right_ref, left_ref, start):
    pairs, _, tile_rows, tile_cols = ref.shape
    row = lax.broadcasted_iota(jnp.int32, (2 * HALO, tile_cols), 0)
    col = lax.broadcasted_iota(jnp.int32, (2 * HALO, tile_cols), 1)
    wanted = jnp.where(row < HALO, row + (tile_cols - HALO), row - HALO)
    pick = (col == wanted).astype(F32).astype(BF16)
    span = pairs * tile_rows
    for image in range(2):
        pixels = ref[:, image].reshape(span, tile_cols)
        taken = dot(pick, pixels, ((1,), (1,))).astype(BF16)
        place = slice(start + image * span, start + (image + 1) * span)
        right_ref[:, place] = taken[:HALO]
        left_ref[:, place] = taken[HALO:]


def strips_kernel(up_ref, own_right_ref, own_left_ref, down_ref, right_ref, left_ref):
    width = own_right_ref.shape[1]
    take_strips(up_ref, right_ref, left_ref, 0)
    right_ref[:, width : 2 * width] = own_right_ref[...]
    left_ref[:, width : 2 * width] = own_left_ref[...]
    take_strips(down_ref, right_ref, left_ref, 2 * width)


def fetch(sources, targets, sems):
    copies = [pltpu.make_async_copy(a, b, sems.at[i]) for i, (a, b) in enumerate(zip(sources, targets))]
    for copy in copies:
        copy.start()
    return copies


def weights_kernel(
    shift_hbm,
    phase_hbm,
    frames_hbm,
    rows_hbm,
    cols_hbm,
    table_hbm,
    moved_ref,
    bins_ref,
    own_ref,
    high_ref,
    low_ref,
    ehigh_ref,
    elow_ref,
    rhigh_ref,
    rlow_ref,
    right_ref,
    left_ref,
    shift_ref,
    rows_ref,
    cols_ref,
    table_ref,
    wide_ref,
    sems,
):
    copies = fetch(
        (shift_hbm, rows_hbm, cols_hbm, table_hbm, shift_hbm, phase_hbm, frames_hbm),
        (shift_ref, rows_ref, cols_ref, table_ref, moved_ref, bins_ref, own_ref),
        sems,
    )
    windows = shift_ref.shape[2]
    lanes = wide_ref.shape[2]
    for copy in copies[:4]:
        copy.wait()
    packed, turned = table_ref[:, : 2 * lanes], table_ref[:, 2 * lanes :]
    column = dot(cols_ref[...], packed, ((0,), (0,)))
    column = jnp.concatenate([column, jnp.zeros((40 - PATCH, 2 * lanes), F32)], axis=0)
    wide_ref[...] = jnp.zeros_like(wide_ref)
    owner = lax.broadcasted_iota(jnp.int32, (40, lanes), 1) // SLOTS
    for w in range(windows):
        start = STEP * w + HALO - (WIN - STEP) // 2 - BAND + shift_ref[1, 0, w]
        rows = pl.ds(start, 40)
        for t in range(2):
            wide_ref[t, rows, :] = jnp.where(
                owner == w, column[:, t * lanes : (t + 1) * lanes], wide_ref[t, rows, :]
            )
    inner = slice(HALO, HALO + high_ref.shape[0])
    right = slice(inner.stop, inner.stop + HALO)
    lane = lax.broadcasted_iota(jnp.int32, (1, lanes), 1)
    for t in range(2):
        place = slice(t * lanes, (t + 1) * lanes)
        values = wide_ref[t, inner, :]
        high = values.astype(BF16)
        high_ref[:, place] = high
        low_ref[:, place] = (values - high.astype(F32)).astype(BF16)
        values = jnp.concatenate([values, wide_ref[t, :HALO, :], wide_ref[t, right, :]], axis=0)
        ends = jnp.where(lane < SLOTS, values, 0.0) + jnp.where(
            lane // SLOTS == 1, pltpu.roll(values, 2 * SLOTS, 1), 0.0
        )
        for h in range(QUARTERS):
            placed = ends if h == 0 else pltpu.roll(ends, 2 * SLOTS * h, 1)
            high = placed.astype(BF16)
            ehigh_ref[h, :, place] = high
            elow_ref[h, :, place] = (placed - high.astype(F32)).astype(BF16)
    place = lax.broadcasted_iota(jnp.int32, (PATCH, GROUP * SPAN), 1) % SPAN
    spread = (place == lax.broadcasted_iota(jnp.int32, (PATCH, GROUP * SPAN), 0)).astype(F32).astype(BF16)
    spread = dot(rows_ref[...], spread).astype(BF16)
    left = dot(turned, spread, ((0,), (0,)))
    mine = (lax.broadcasted_iota(jnp.int32, left.shape, 0) // WIN) % GROUP
    theirs = lax.broadcasted_iota(jnp.int32, left.shape, 1) // SPAN
    left = jnp.where(mine == theirs, left, 0.0)
    high = left.astype(BF16)
    rhigh_ref[...] = high
    rlow_ref[...] = (left - high.astype(F32)).astype(BF16)
    for copy in copies[4:]:
        copy.wait()
    take_strips(own_ref, right_ref, left_ref, 0)


def starts(shift_ref, windows):
    return [HALO - (WIN - STEP) // 2 - BAND + shift_ref[0, 0, w] for w in windows]


def cross_spectra(half_a, half_b, pairs, offsets, owner, left_ref, rhigh_ref, rlow_ref):
    lanes = half_b.shape[3]
    head = (half_a.shape[1] - WIN) // 2
    zero_slot = lax.broadcasted_iota(jnp.int32, (1, lanes), 1) % SLOTS == 0
    first_row = lax.broadcasted_iota(jnp.int32, (GROUP * WIN, 1), 0) % WIN == 0
    part_a, part_b = [], []
    for p in pairs:
        real = half_a[p, head : head + WIN, :lanes]
        mean = jnp.sum(real, axis=0, keepdims=True) * (1.0 / WIN)
        real = real - jnp.where(zero_slot, mean, 0.0)
        part_a.append(jnp.concatenate([real, half_a[p, head : head + WIN, lanes:]], axis=1))
        lined = []
        for t in range(2):
            taken = half_b[t, p, pl.ds(offsets[0], SPAN), :]
            for w in range(1, len(offsets)):
                taken = jnp.where(owner == w, half_b[t, p, pl.ds(offsets[w], SPAN), :], taken)
            lined.append(taken)
        part_b.append(jnp.concatenate(lined, axis=1))
    rows_a = jnp.concatenate(part_a, axis=0).astype(BF16)
    rows_b = jnp.concatenate(part_b, axis=0)
    high = rows_b.astype(BF16)
    low = (rows_b - high.astype(F32)).astype(BF16)
    spec_a = dot(left_ref[...], rows_a)
    spec_b = dot(rhigh_ref[...], high) + dot(rhigh_ref[...], low) + dot(rlow_ref[...], high)
    half_rows = GROUP * WIN
    a_cr, a_ci = spec_a[:half_rows, :lanes], spec_a[:half_rows, lanes:]
    a_sr, a_si = spec_a[half_rows:, :lanes], spec_a[half_rows:, lanes:]
    b_cr, b_ci = spec_b[:half_rows, :lanes], spec_b[:half_rows, lanes:]
    b_sr, b_si = spec_b[half_rows:, :lanes], spec_b[half_rows:, lanes:]
    b_cr = jnp.where(zero_slot & first_row, 0.0, b_cr)
    a_real, a_imag = a_cr + jnp.where(zero_slot, 0.0, a_si), jnp.where(zero_slot, 0.0, a_ci) - a_sr
    b_real, b_imag = b_cr + jnp.where(zero_slot, 0.0, b_si), jnp.where(zero_slot, 0.0, b_ci) - b_sr
    last_real = jnp.where(zero_slot, a_ci * b_ci + a_si * b_si, 0.0)
    last_imag = jnp.where(zero_slot, a_si * b_ci - a_ci * b_si, 0.0)
    cross_real = a_real * b_real + a_imag * b_imag - last_imag
    cross_imag = a_real * b_imag - a_imag * b_real + last_real
    return cross_real, cross_imag


def inner_kernel(
    phase_vec,
    shift_vec,
    own_ref,
    up_ref,
    down_ref,
    first_ref,
    high_ref,
    low_ref,
    left_ref,
    rhigh_ref,
    rlow_ref,
    sums,
    half_a,
    half_b,
    phase_ref,
    shift_ref,
    sems,
):
    copies = fetch((phase_vec, shift_vec), (phase_ref, shift_ref), sems)
    pairs, _, tile_rows, tile_cols = own_ref.shape
    windows = shift_ref.shape[2]
    lanes = windows * SLOTS
    span = pairs * tile_rows
    for at, ref in enumerate((up_ref, own_ref, down_ref)):
        rows = slice(at * tile_rows, (at + 1) * tile_rows)
        pixels = ref[:, 0].reshape(span, tile_cols)
        half_a[:, rows, :] = dot(pixels, first_ref[...]).reshape(pairs, tile_rows, 2 * lanes)
        pixels = ref[:, 1].reshape(span, tile_cols)
        half = dot(pixels, high_ref[...]) + dot(pixels, low_ref[...])
        for t in range(2):
            half_b[t, :, rows, :] = half[:, t * lanes : (t + 1) * lanes].reshape(pairs, tile_rows, lanes)
    half_b[:, :, 3 * tile_rows :, :] = jnp.zeros((2, pairs, half_b.shape[2] - 3 * tile_rows, lanes), F32)
    sums[...] = jnp.zeros_like(sums)
    owner = lax.broadcasted_iota(jnp.int32, (1, lanes), 1) // SLOTS
    for copy in copies:
        copy.wait()
    offsets = starts(shift_ref, range(windows))
    for g in range(pairs // GROUP):
        members = range(g * GROUP, (g + 1) * GROUP)
        real, imag = cross_spectra(half_a, half_b, members, offsets, owner, left_ref, rhigh_ref, rlow_ref)
        for q, p in enumerate(members):
            b = phase_ref[p]
            rows = slice(q * WIN, (q + 1) * WIN)
            sums[b, :, :lanes] += real[rows]
            sums[b, :, lanes:] += imag[rows]


def edge_kernel(
    phase_vec,
    shift_vec,
    own_ref,
    up_ref,
    down_ref,
    before_ref,
    after_ref,
    first_ref,
    high_ref,
    low_ref,
    left_ref,
    rhigh_ref,
    rlow_ref,
    inner_ref,
    out_ref,
    half_a,
    half_b,
    sums,
    phase_ref,
    shift_ref,
    sems,
):
    copies = fetch((phase_vec, shift_vec), (phase_ref, shift_ref), sems)
    pairs, _, tile_rows, tile_cols = own_ref.shape
    windows = shift_ref.shape[2]
    lanes = windows * SLOTS
    span = pairs * tile_rows
    part = span // QUARTERS
    each = pairs // QUARTERS

    def along_columns(pixels, weights_ref):
        total = dot(pixels[:part], weights_ref[0])
        for h in range(1, QUARTERS):
            total = total + dot(pixels[h * part : (h + 1) * part], weights_ref[h])
        return total

    for at, ref in enumerate((up_ref, own_ref, down_ref)):
        rows = slice(at * tile_rows, (at + 1) * tile_rows)
        taken = []
        for image in range(2):
            place = slice((2 * at + image) * span, (2 * at + image + 1) * span)
            strip = jnp.concatenate([before_ref[:, place], after_ref[:, place]], axis=0)
            strip = jnp.transpose(strip.astype(F32)).astype(BF16)
            taken.append(jnp.concatenate([ref[:, image].reshape(span, tile_cols), strip], axis=1))
        half_a[:, rows, :] = along_columns(taken[0], first_ref).reshape(each, tile_rows, 2 * lanes)
        half = along_columns(taken[1], high_ref) + along_columns(taken[1], low_ref)
        for t in range(2):
            half_b[t, :, rows, :] = half[:, t * lanes : (t + 1) * lanes].reshape(each, tile_rows, lanes)
    half_b[:, :, 3 * tile_rows :, :] = jnp.zeros((2, each, half_b.shape[2] - 3 * tile_rows, lanes), F32)
    sums[...] = jnp.zeros_like(sums)
    lane = lax.broadcasted_iota(jnp.int32, (1, lanes), 1)
    for copy in copies:
        copy.wait()
    offsets = starts(shift_ref, (0, windows - 1))
    real, imag = cross_spectra(
        half_a, half_b, range(each), offsets, (lane // SLOTS) % 2, left_ref, rhigh_ref, rlow_ref
    )
    for q in range(each):
        rows = slice(q * WIN, (q + 1) * WIN)
        for h in range(QUARTERS):
            b = phase_ref[h * each + q]
            mine = lane // (2 * SLOTS) == h
            sums[b, :, :lanes] += jnp.where(mine, real[rows], 0.0)
            sums[b, :, lanes:] += jnp.where(mine, imag[rows], 0.0)
    edge = (lane < SLOTS) | (lane >= lanes - SLOTS)
    for b in range(sums.shape[0]):
        for t in range(2):
            place = slice(t * lanes, (t + 1) * lanes)
            total = sums[b, :, place]
            total = total + pltpu.roll(total, lanes // 2, 1)
            total = total + pltpu.roll(total, lanes // 4, 1)
            out_ref[b, :, place] = jnp.where(edge, total, inner_ref[b, :, place]).astype(BF16)


def split(values):
    high = values.astype(BF16)
    return high, (values - high.astype(F32)).astype(BF16)


def fine_dot(a, b):
    a_high, a_low = split(a)
    b_high, b_low = split(b)
    return dot(a_high, b_high) + (dot(a_high, b_low) + dot(a_low, b_high))


def inverse_kernel(parts_ref, rows_ref, places_ref, out_ref, lines):
    windows = out_ref.shape[0]
    lanes = windows * SLOTS
    total = jnp.sum(parts_ref[...].astype(F32), axis=0)
    turned = fine_dot(rows_ref[...], total)
    lines[:, :lanes] = turned[:WIN, :lanes] - turned[WIN:, lanes:]
    lines[:, lanes:] = turned[WIN:, :lanes] + turned[:WIN, lanes:]
    owner = (lax.broadcasted_iota(jnp.int32, (windows, 2 * lanes), 1) % lanes) // SLOTS
    own = owner == lax.broadcasted_iota(jnp.int32, (windows, 2 * lanes), 0)
    spread = jnp.concatenate(
        [jnp.where(own, jnp.broadcast_to(lines[u : u + 1, :], (windows, 2 * lanes)), 0.0) for u in range(WIN)],
        axis=0,
    )
    planes = fine_dot(spread, places_ref[...])
    for u in range(WIN):
        out_ref[:, u * WIN : (u + 1) * WIN] = planes[u * windows : (u + 1) * windows]


def shifted(values, axis, step):
    count = lax.axis_size(axis)
    return lax.ppermute(values, axis, [(i, i + step) for i in range(count) if 0 <= i + step < count])


def stay(*values):
    return [pltpu.with_memory_space_constraint(jnp.asarray(value), pltpu.HBM) for value in values]


def call(kernel, outs, specs, scratch=(), flops=0, size=0, room=16):
    return pl.pallas_call(
        kernel,
        out_shape=outs,
        in_specs=specs,
        out_specs=jax.tree.map(lambda _: whole(), outs),
        scratch_shapes=scratch,
        compiler_params=pltpu.CompilerParams(vmem_limit_bytes=room << 20),
        cost_estimate=pl.CostEstimate(flops=flops, bytes_accessed=size, transcendentals=0),
    )


def body(frames, phase, shift, interp_rows, interp_cols):
    pairs, _, tile_rows, tile_cols = frames.shape
    windows = tile_cols // STEP
    lanes = windows * SLOTS
    bins = lax.axis_size("tm")
    fixed = constants(windows)
    shape = jax.ShapeDtypeStruct
    vmem, hbm = whole(), whole(pltpu.HBM)

    up = shifted(frames, "row", 1)
    down = shifted(frames, "row", -1)
    wide = 2 * HALO + tile_cols
    strip = shape((HALO, 2 * pairs * tile_rows), BF16)
    scalars = pltpu.SMEM(shift.shape, shift.dtype)
    weights = shape((tile_cols, 2 * lanes), BF16)
    ends = shape((QUARTERS, wide, 2 * lanes), BF16)
    left = shape((2 * GROUP * WIN, GROUP * SPAN), BF16)
    moved, phases, own, high, low, ehigh, elow, rhigh, rlow, own_right, own_left = call(
        weights_kernel,
        (
            shape(shift.shape, shift.dtype),
            shape(phase.shape, phase.dtype),
            shape(frames.shape, BF16),
            weights,
            weights,
            ends,
            ends,
            left,
            left,
            strip,
            strip,
        ),
        [hbm] * 6,
        scratch=[
            scalars,
            pltpu.VMEM(interp_rows.shape, BF16),
            pltpu.VMEM(interp_cols.shape, BF16),
            pltpu.VMEM(fixed["table"].shape, BF16),
            pltpu.VMEM((2, wide + 8, lanes), F32),
            pltpu.SemaphoreType.DMA((7,)),
        ],
        flops=10**7,
        size=400000,
    )(*stay(shift, phase, frames, interp_rows, interp_cols, fixed["table"]))

    side = shape((HALO, 6 * pairs * tile_rows), BF16)
    rightward, leftward = call(strips_kernel, (side, side), [vmem] * 4, flops=10**7, size=200000)(
        up, own_right, own_left, down
    )
    before = shifted(rightward, "col", 1)
    after = shifted(leftward, "col", -1)

    tall = 3 * tile_rows
    fetched = [pltpu.SMEM(phase.shape, phase.dtype), scalars, pltpu.SemaphoreType.DMA((2,))]
    inner = call(
        inner_kernel,
        shape((bins, WIN, 2 * lanes), F32),
        [vmem] * 11,
        scratch=[pltpu.VMEM((pairs, tall, 2 * lanes), F32), pltpu.VMEM((2, pairs, tall + 8, lanes), F32)] + fetched,
        flops=10**9,
        size=10**6,
    )(phases, moved, own, up, down, fixed["own"], high, low, fixed["left_a"], rhigh, rlow)
    each = pairs // QUARTERS
    partial_sums = call(
        edge_kernel,
        shape((bins, WIN, 2 * lanes), BF16),
        [vmem] * 14,
        scratch=[
            pltpu.VMEM((each, tall, 2 * lanes), F32),
            pltpu.VMEM((2, each, tall + 8, lanes), F32),
            pltpu.VMEM((bins, WIN, 2 * lanes), F32),
        ]
        + fetched,
        flops=10**9,
        size=10**6,
    )(
        phases,
        moved,
        own,
        up,
        down,
        before,
        after,
        fixed["edges"],
        ehigh,
        elow,
        fixed["left_a"],
        rhigh,
        rlow,
        inner,
    )
    parts = lax.all_to_all(partial_sums, "tm", 0, 0, tiled=True)
    planes = call(
        inverse_kernel,
        shape((windows, WIN * WIN), F32),
        [vmem] * 3,
        scratch=[pltpu.VMEM((WIN, 2 * lanes), F32)],
        flops=10**8,
        size=10**6,
    )(parts, fixed["inverse_rows"], fixed["places"])
    return planes[None, None]


def solution(mesh):
    placed = (P("tm", None, "row", "col"), P("tm"), P(None, "row", "col"), P(), P())
    return jax.shard_map(
        body, mesh=mesh, in_specs=placed, out_specs=P("tm", "row", "col", None), check_vma=False
    )
```
